32 devices in a mesh: section: 2 (over x), chan: 16 (over z, y, core).
Axes of the slice: x: 2, y: 2, z: 4, core: 2. Of those that a mesh axis runs over, the one named last changes fastest.
Arguments:
- raw_strain: float32 [1024, 20480], P('chan', 'section'), may hold values from -6 to 6
- seg_starts: int32 [16], P('section'), may hold values from 0 to 8192, as said below
- quality_mask: int32 [16, 1024], P(None, 'chan'), may hold values 0 or 1
- pair_reach: int32 [1024], P('chan'), may hold values from 224 to 448
Outputs:
- correlations: bfloat16 [1024, 102912], P('chan', 'section')
The draws below stay inside these ranges and needn't reach their ends.
Inputs may be any that keep to these rules, and one draw needn't show every extreme that they name: `seg_starts`: segment k starts 1024 * (k mod 8) plus 0 to 1024 samples into its sub-window.
All inputs are finite; a program needn't handle non-finite values. No bound on the sum of `quality_mask` on one device may be relied on, other than what follows from the above.
Results may differ from the reference program's by a relative error of at most 0.0072.
Values may be sent and summed in bfloat16 or wider, within the bound.
A program may use at most 192 MiB of HBM per device.

```python
import math
import jax
import jax.numpy as jnp
from jax import lax

SEG = 2048
F = 1024
HOP = 1024
SMOOTH = 64
MAXLAG = 100
LAGS = 201
CH_DEV = 64
STOPS = 8
SEG_DEV = 8
NSEG = 16
RAW_DEV = 10240
RAW = 20480
CHANNELS = 1024
BAND = 448


def draw_seg_starts(key, part):
    jitter = jax.random.randint(key, (NSEG,), 0, HOP + 1)
    nominal = jnp.arange(NSEG, dtype=jnp.int32) % SEG_DEV * HOP
    starts_all = (nominal + jitter).astype(jnp.int32)
    starts_all = starts_all.at[0].set(0)
    starts_all = starts_all.at[NSEG - 1].set(RAW_DEV - SEG)
    return starts_all.astype(jnp.int32)


def draw_pair_reach(key, part):
    reach_all = jax.random.randint(key, (CHANNELS,), BAND // 2, BAND + 1)
    where_top = jax.random.randint(jax.random.fold_in(key, 7), (), 0, CHANNELS)
    reach_all = reach_all.at[where_top].set(BAND)
    return reach_all.astype(jnp.int32)


def touch_ends(values, own_key, smallest, largest):
    spot = [jax.random.randint(jax.random.fold_in(own_key, axis), (), 0, length) for axis, length in enumerate(values.shape)]
    widest = values.shape.index(max(values.shape))
    next_to = spot[:widest] + [(spot[widest] + 1) % values.shape[widest]] + spot[widest + 1:]
    return values.at[tuple(spot)].set(smallest).at[tuple(next_to)].set(largest)


def block_levels(stream_key, extent, split, smallest, top_value):
    gain = 1.0
    for axis_at, parts in split:
        steps = jax.random.uniform(jax.random.fold_in(jax.random.fold_in(stream_key, 6), axis_at), (parts,), jnp.float32, smallest / len(split), top_value / len(split))
        gain = gain * jnp.repeat(jnp.exp(steps), extent[axis_at] // parts).reshape((-1,) + (1,) * (len(extent) - 1 - axis_at))
    return gain


def bell_draw(stream_key, shape, deviation, bound, shards=(), kind=jnp.bfloat16):
    drawn = jax.random.normal(stream_key, shape, jnp.float32) * deviation
    if len(shards) > 0:
        drawn = block_levels(stream_key, shape, shards, -0.22, 0.18) * drawn
    return jnp.clip(drawn, min=-bound, max=bound).astype(kind)


def setup_inputs(seed: int = 0) -> dict:
    key_list = jax.random.split(jax.random.key(seed), 5)
    return {
        "raw_strain": bell_draw(key_list[0], (CHANNELS, RAW), 1.0, 6.0, ((0, 16), (1, 2)), jnp.float32),
        "seg_starts": draw_seg_starts(jax.random.fold_in(key_list[4], 71), 0),
        "quality_mask": touch_ends((jax.random.randint(key_list[2], (NSEG, CHANNELS), 0, 5) < 3).astype(jnp.int32), jax.random.fold_in(key_list[2], 1), 0, 1),
        "pair_reach": draw_pair_reach(jax.random.fold_in(key_list[4], 71), 0),
    }


def hann_window():
    steps = jnp.arange(SEG, dtype=jnp.int32).astype(jnp.float32)
    return 0.5 - 0.5 * jnp.cos(2.0 * math.pi / SEG * steps)

def dft_table():
    times = jnp.arange(SEG, dtype=jnp.int32)[:, None]
    freqs = jnp.arange(F, dtype=jnp.int32)[None, :]
    angle = 2.0 * math.pi / SEG * (times * freqs % SEG).astype(jnp.float32)
    return jnp.concatenate([jnp.cos(angle), -jnp.sin(angle)], axis=1).astype(jnp.bfloat16)

def band_matrix():
    source = jnp.arange(F, dtype=jnp.int32)[:, None]
    target = jnp.arange(F, dtype=jnp.int32)[None, :]
    inside = jnp.abs(source - target) <= SMOOTH
    counted = (jnp.minimum(target + SMOOTH, F - 1) - jnp.maximum(target - SMOOTH, 0) + 1).astype(jnp.float32)
    return jnp.where(inside, 1.0 / counted, 0.0).astype(jnp.float32)

def lag_table(freq_start, freq_count):
    freqs = (freq_start + jnp.arange(freq_count, dtype=jnp.int32))[:, None]
    shifts = (jnp.arange(LAGS, dtype=jnp.int32) - MAXLAG)[None, :]
    angle = 2.0 * math.pi / SEG * (freqs * shifts % SEG).astype(jnp.float32)
    factor = 1.0 / math.sqrt(F)
    return jnp.concatenate([jnp.cos(angle) * factor, -jnp.sin(angle) * factor], axis=0).astype(jnp.bfloat16)

def pair_valid(block_idx, stop_idx, num_chan, total_chan, reach):
    rows = jnp.arange(num_chan, dtype=jnp.int32)
    first_chan = block_idx * num_chan + rows
    second_chan = (block_idx + stop_idx) * num_chan + rows
    offset_gap = second_chan[None, :] - first_chan[:, None]
    keep = (offset_gap >= 1) & (offset_gap <= reach[:, None]) & (second_chan[None, :] < total_chan)
    return keep.astype(jnp.float32)

def correlate(own_spec, blk_spec, own_mask, blk_mask, lag_tab, valid_pairs):
    own_spec = own_spec.astype(jnp.float32)
    blk_spec = blk_spec.astype(jnp.float32)
    own_pair = jnp.concatenate([own_spec[:, :, 0], own_spec[:, :, 1]], axis=1)
    own_turn = jnp.concatenate([own_spec[:, :, 1], -own_spec[:, :, 0]], axis=1)
    blk_pair = jnp.concatenate([blk_spec[:, :, 0], blk_spec[:, :, 1]], axis=1)
    cross_re = jnp.einsum('ikf,jkf->ijf', own_pair, blk_pair, precision=lax.Precision.HIGHEST)
    cross_im = jnp.einsum('ikf,jkf->ijf', own_turn, blk_pair, precision=lax.Precision.HIGHEST)
    counts = jnp.dot(own_mask.astype(jnp.float32).T, blk_mask.astype(jnp.float32), precision=lax.Precision.HIGHEST)
    divisor = jnp.maximum(counts, 1.0)[:, :, None]
    stacked = jnp.concatenate([cross_re / divisor, cross_im / divisor], axis=2).astype(jnp.bfloat16)
    rows_a = stacked.shape[0]
    rows_b = stacked.shape[1]
    lagged = jnp.dot(stacked.reshape(rows_a * rows_b, -1), lag_tab, preferred_element_type=jnp.float32)
    return lagged.reshape(rows_a, rows_b, -1) * valid_pairs[:, :, None]

def reference(raw_strain, seg_starts, quality_mask, pair_reach):
    n_block = CHANNELS // CH_DEV
    offsets = (jnp.arange(NSEG, dtype=jnp.int32) // SEG_DEV * RAW_DEV + seg_starts.astype(jnp.int32)).astype(jnp.int32)
    dft = dft_table()
    band = band_matrix()
    window_shape = hann_window()
    mask_f = quality_mask.astype(jnp.float32)

    def spectra_of(block):
        start_row = (block * CH_DEV).astype(jnp.int32)
        strain_rows = lax.dynamic_slice_in_dim(raw_strain, start_row, CH_DEV, 0)
        windows = jax.vmap(lambda offset: lax.dynamic_slice_in_dim(strain_rows, offset, SEG, 1), out_axes=1)(offsets)
        centred = windows - lax.optimization_barrier(jnp.mean(windows, axis=2, keepdims=True))
        tapered = (centred * window_shape).astype(jnp.bfloat16)
        spectrum = jnp.dot(tapered.reshape(CH_DEV * NSEG, SEG), dft, preferred_element_type=jnp.float32)
        real_part = spectrum[:, :F]
        imag_part = spectrum[:, F:]
        smooth = jnp.dot(real_part * real_part + imag_part * imag_part, band, precision=lax.Precision.HIGHEST)
        scale_den = jnp.sqrt(smooth + 1e-06)
        block_mask = lax.dynamic_slice_in_dim(mask_f, start_row, CH_DEV, 1).T.reshape(-1, 1)
        real_w = real_part / scale_den * block_mask
        imag_w = imag_part / scale_den * block_mask
        return jnp.stack([real_w, imag_w], axis=1).astype(jnp.bfloat16).reshape(CH_DEV, NSEG, 2, F)
    all_spec = lax.map(spectra_of, jnp.arange(n_block, dtype=jnp.int32))
    padded_spec = jnp.concatenate([all_spec, jnp.zeros((STOPS, CH_DEV, NSEG, 2, F), jnp.bfloat16)], axis=0)
    block_masks = mask_f.reshape(NSEG, n_block, CH_DEV).transpose(1, 0, 2)
    padded_mask = jnp.concatenate([block_masks, jnp.zeros((STOPS, NSEG, CH_DEV), jnp.float32)], axis=0)
    lag_tab = lag_table(0, F)

    def per_block(block):
        own_spec = padded_spec[block]
        own_mask = padded_mask[block]
        reach = lax.dynamic_slice_in_dim(pair_reach, (block * CH_DEV).astype(jnp.int32), CH_DEV, 0)

        def per_stop(stop_idx):
            valid_pairs = pair_valid(block, stop_idx, CH_DEV, CHANNELS, reach)
            other = (block + stop_idx).astype(jnp.int32)
            lagged = correlate(own_spec, padded_spec[other], own_mask, padded_mask[other], lag_tab, valid_pairs)
            return lagged.astype(jnp.bfloat16)
        return lax.map(per_stop, jnp.arange(STOPS, dtype=jnp.int32)).transpose(1, 0, 2, 3)
    result = lax.map(per_block, jnp.arange(n_block, dtype=jnp.int32))
    return result.reshape(CHANNELS, STOPS * CH_DEV * LAGS)
```

```python
import math

import jax
import jax.numpy as jnp
from jax import lax
from jax.experimental import pallas as pl
from jax.experimental.pallas import tpu as pltpu
from jax.sharding import PartitionSpec as P

SEG = 2048
F = 1024
SMOOTH = 64
MAXLAG = 100
LAGS = 201
STOPS = 8


def hann_window():
    steps = jnp.arange(SEG, dtype=jnp.int32).astype(jnp.float32)
    return 0.5 - 0.5 * jnp.cos(2.0 * math.pi / SEG * steps)


def dft_rows():
    freqs = jnp.arange(F, dtype=jnp.int32)[:, None]
    times = jnp.arange(SEG, dtype=jnp.int32)[None, :]
    angle = 2.0 * math.pi / SEG * (times * freqs % SEG).astype(jnp.float32)
    return jnp.concatenate([jnp.cos(angle), -jnp.sin(angle)], axis=0).astype(jnp.bfloat16)


def band_rows():
    target = jnp.arange(F, dtype=jnp.int32)[:, None]
    source = jnp.arange(F, dtype=jnp.int32)[None, :]
    inside = jnp.abs(source - target) <= SMOOTH
    counted = (jnp.minimum(target + SMOOTH, F - 1) - jnp.maximum(target - SMOOTH, 0) + 1).astype(
        jnp.float32
    )
    return jnp.where(inside, 1.0 / counted, 0.0)


GROUP = 8
LAG_ROWS = 208
ROWS = 32
STEPS = 8


def lag_rows():
    freqs = jnp.arange(F, dtype=jnp.int32)[None, :]
    shifts = (jnp.arange(LAG_ROWS, dtype=jnp.int32) - MAXLAG)[:, None]
    angle = 2.0 * math.pi / SEG * (freqs * shifts % SEG).astype(jnp.float32)
    factor = 1.0 / math.sqrt(F)
    both = jnp.stack([jnp.cos(angle) * factor, -jnp.sin(angle) * factor], axis=1)
    both = jnp.where(shifts[:, :, None] <= MAXLAG, both, 0.0)
    both = both.reshape(LAG_ROWS, 2, F // GROUP, GROUP).transpose(0, 2, 1, 3)
    return both.reshape(LAG_ROWS, 2 * F).astype(jnp.bfloat16)


def correlate_kernel(*refs):
    pair_ref, turn_ref = refs[0], refs[1]
    blocks = refs[2:10]
    lag_ref, scale_ref, out_ref, cross, lagged = refs[10:]
    step = pl.program_id(1)
    rows = pair_ref.shape[2]
    depth = pair_ref.shape[3]
    groups = pair_ref.shape[1]
    half_depth = depth // 2
    per_freq = half_depth // GROUP
    chans = blocks[0].shape[1] // 2
    cols = 4 * chans
    lane = lax.broadcasted_iota(jnp.int32, (GROUP, depth), 1)
    row = lax.broadcasted_iota(jnp.int32, (GROUP, depth), 0)
    keep = (lax.rem(lane, half_depth) // per_freq == row)[None]

    def one_group(g, carry):
        at = pl.multiple_of(g * half_depth, half_depth)
        tiles = [ref[pl.ds(at, half_depth), :] for ref in blocks]
        for fh in range(2):
            cut = slice(fh * chans, (fh + 1) * chans)
            mine = jnp.concatenate([t[:, cut] for t in tiles[:4]], axis=1)
            other = jnp.concatenate([t[:, cut] for t in tiles[4:]], axis=1)
            weights = jnp.concatenate([mine, other], axis=0)
            pair = pair_ref[fh, g].astype(jnp.float32)[:, None, :]
            turn = turn_ref[fh, g].astype(jnp.float32)[:, None, :]
            spread = jnp.concatenate(
                [jnp.where(keep, pair, 0.0), jnp.where(keep, turn, 0.0)], axis=1
            )
            spread = spread.reshape(rows * 2 * GROUP, depth).astype(jnp.bfloat16)
            product = jnp.dot(spread, weights, preferred_element_type=jnp.float32)
            place = (fh * groups * pl.num_programs(1) + step * groups + g) * 2 * GROUP
            cross[:, pl.ds(pl.multiple_of(place, 2 * GROUP), 2 * GROUP), :] = product.astype(
                jnp.bfloat16
            ).reshape(rows, 2 * GROUP, cols)
        return carry

    lax.fori_loop(0, groups, one_group, 0)

    @pl.when(step == pl.num_programs(1) - 1)
    def finish():
        def one_row(i, carry):
            value = jnp.dot(lag_ref[...], cross[i], preferred_element_type=jnp.float32)
            value = value * scale_ref[pl.ds(i, 1), :]
            value = jnp.concatenate(
                [value, jnp.zeros((256 - LAG_ROWS, cols), jnp.float32)], axis=0
            )
            lagged[:, pl.ds(i, 1), :] = value.T[:, None, :]
            return carry

        lax.fori_loop(0, rows, one_row, 0)
        lanes = lax.broadcasted_iota(jnp.int32, (rows, 128), 1)

        def span(h, carry):
            base = h * 128
            out_at = h * (128 * LAGS)
            waiting = {}
            for j in range(128):
                tile, shift = divmod(j * LAGS, 128)
                block = lagged[base + j]
                if shift:
                    block = pltpu.roll(block, shift, 1)
                first, second = block[:, :128], block[:, 128:]
                if shift:
                    parts = (
                        jnp.where(lanes >= shift, first, 0.0),
                        second,
                        jnp.where(lanes < shift, first, 0.0),
                    )
                else:
                    parts = (first, second)
                for t, part in enumerate(parts):
                    have = waiting.get(tile + t)
                    waiting[tile + t] = part if have is None else have + part
                upto = (j + 1) * LAGS // 128
                for t in sorted(waiting):
                    if t < upto:
                        done = waiting.pop(t)
                        out_ref[:, pl.ds(pl.multiple_of(out_at + t * 128, 128), 128)] = (
                            done.astype(out_ref.dtype)
                        )
            return carry

        lax.fori_loop(0, cols // 128, span, 0)


def correlate(pair, turn, blocks, lags, scale):
    num_chan = pair.shape[2]
    rows = min(ROWS, num_chan)
    groups = pair.shape[1] // STEPS
    block_rows = blocks[0].shape[0] // STEPS
    cols = scale.shape[1]
    own_spec = pl.BlockSpec((2, groups, rows, pair.shape[3]), lambda i, g: (0, g, i, 0))
    blk_spec = pl.BlockSpec((block_rows, 2 * num_chan), lambda i, g: (g, 0))
    return pl.pallas_call(
        correlate_kernel,
        grid=(num_chan // rows, STEPS),
        out_shape=jax.ShapeDtypeStruct((num_chan, cols * LAGS), jnp.bfloat16),
        in_specs=[own_spec, own_spec]
        + [blk_spec] * 8
        + [
            pl.BlockSpec((LAG_ROWS, 2 * F), lambda i, g: (0, 0)),
            pl.BlockSpec((rows, cols), lambda i, g: (i, 0)),
        ],
        out_specs=pl.BlockSpec((rows, cols * LAGS), lambda i, g: (i, 0)),
        scratch_shapes=[
            pltpu.VMEM((rows, 2 * F, cols), jnp.bfloat16),
            pltpu.VMEM((cols, rows, 256), jnp.float32),
        ],
        compiler_params=pltpu.CompilerParams(vmem_limit_bytes=67043328 - 1024 * 1024),
    )(pair, turn, *blocks, lags, scale)


def swap_section(value):
    count = lax.axis_size("section")
    return lax.ppermute(value, "section", [(i, count - 1 - i) for i in range(count)])


def fetch(value, route):
    return lax.ppermute(value, "chan", route)


def shards(raw_strain, seg_starts, quality_mask, pair_reach):
    num_chan = raw_strain.shape[0]
    seg_local = seg_starts.shape[0]
    section_idx = lax.axis_index("section")
    chan_idx = lax.axis_index("chan")
    cycle_size = lax.axis_size("chan")
    total_chan = num_chan * cycle_size
    windows = jax.vmap(
        lambda offset: lax.dynamic_slice_in_dim(raw_strain, offset, SEG, 1), out_axes=0
    )(seg_starts)
    centred = windows - jnp.mean(windows, axis=2, keepdims=True)
    tapered = (centred * hann_window()).astype(jnp.bfloat16)
    spectrum = lax.dot_general(
        dft_rows(),
        tapered.reshape(seg_local * num_chan, SEG),
        (((1,), (1,)), ((), ())),
        preferred_element_type=jnp.float32,
    )
    real_part = spectrum[:F]
    imag_part = spectrum[F:]
    smooth = jnp.dot(
        band_rows(), real_part * real_part + imag_part * imag_part, precision=lax.Precision.HIGHEST
    )
    own_rows = lax.dynamic_slice_in_dim(quality_mask, section_idx * seg_local, seg_local, 0).astype(
        jnp.float32
    )
    gain = own_rows.reshape(1, seg_local * num_chan) / jnp.sqrt(smooth + 1e-06)
    white = jnp.stack([real_part * gain, imag_part * gain], axis=1).astype(jnp.bfloat16)
    own = (
        white.reshape(2, F // 2, 2 * seg_local, num_chan)
        .transpose(1, 2, 0, 3)
        .reshape(F * seg_local, 2 * num_chan)
    )

    first = section_idx == 0
    odd_pair = (chan_idx // 2) % 2 == 1
    odd = chan_idx % 2 == 1
    chans = range(cycle_size)
    up4 = [(i, i - 4) for i in chans if i >= 4]
    pair_swap = [(i, i ^ 2) for i in chans]
    core_swap = [(i, i ^ 1) for i in chans]
    own_far = swap_section(own)
    plus4 = fetch(own, up4)
    plus8 = fetch(plus4, up4)
    plus2 = fetch(jnp.where(odd_pair, own, plus4), pair_swap)
    plus6 = fetch(jnp.where(odd_pair, plus4, plus8), pair_swap)
    a0 = jnp.where(first, own, plus4)
    a0_far = swap_section(jnp.where(first, plus4, own))
    a2 = jnp.where(first, plus2, plus6)
    a2_far = swap_section(jnp.where(first, plus6, plus2))
    a4 = jnp.where(first, plus4, plus8)
    a4_far = swap_section(jnp.where(first, plus8, plus4))
    b1 = fetch(jnp.where(odd, a0, a2), core_swap)
    b1_far = fetch(jnp.where(odd, a0_far, a2_far), core_swap)
    b3 = fetch(jnp.where(odd, a2, a4), core_swap)
    b3_far = fetch(jnp.where(odd, a2_far, a4_far), core_swap)

    halves = jnp.stack([own, own_far]).reshape(
        2, F // 2 // GROUP, GROUP, 2, seg_local, 2, num_chan
    )
    turned = jnp.stack([halves[:, :, :, 1], -halves[:, :, :, 0]], axis=3)

    def own_side(value):
        return value.transpose(5, 1, 6, 0, 2, 3, 4).reshape(
            2, F // 2 // GROUP, num_chan, 4 * GROUP * seg_local
        )

    stops_here = STOPS // lax.axis_size("section")
    stop_start = section_idx * stops_here
    wide = lax.all_gather(quality_mask, "chan", axis=1, tiled=True)
    wide = jnp.pad(wide, ((0, 0), (0, STOPS * num_chan))).astype(jnp.float32)
    first_col = (chan_idx + stop_start) * num_chan
    other_mask = lax.dynamic_slice_in_dim(wide, first_col, stops_here * num_chan, 1)
    counts = jnp.dot(
        quality_mask.astype(jnp.float32).T, other_mask, preferred_element_type=jnp.float32
    )
    first_chan = chan_idx * num_chan + jnp.arange(num_chan, dtype=jnp.int32)
    second_chan = first_col + jnp.arange(stops_here * num_chan, dtype=jnp.int32)
    gap = second_chan[None, :] - first_chan[:, None]
    valid = (gap >= 1) & (gap <= pair_reach[:, None]) & (second_chan[None, :] < total_chan)
    scale = jnp.where(valid, 1.0 / jnp.maximum(counts, 1.0), 0.0)

    return correlate(
        own_side(halves),
        own_side(turned),
        (a0, b1, a2, b3, a0_far, b1_far, a2_far, b3_far),
        lag_rows(),
        scale,
    )


def solution(mesh):
    placed = (P("chan", "section"), P("section"), P(None, "chan"), P("chan"))
    return jax.shard_map(
        shards, mesh=mesh, in_specs=placed, out_specs=P("chan", "section"), check_vma=False
    )
```

```python
import math

import jax
import jax.numpy as jnp
from jax import lax
from jax.experimental import pallas as pl
from jax.experimental.pallas import tpu as pltpu
from jax.sharding import PartitionSpec as P

SEG = 2048
F = 1024
SMOOTH = 64
MAXLAG = 100
LAGS = 201
STOPS = 8


def hann_window():
    steps = jnp.arange(SEG, dtype=jnp.int32).astype(jnp.float32)
    return 0.5 - 0.5 * jnp.cos(2.0 * math.pi / SEG * steps)


def turn_table(times, freqs):
    angle = 2.0 * math.pi / SEG * (times * freqs % SEG).astype(jnp.float32)
    return jnp.cos(angle), jnp.sin(angle)


def dft_rows():
    fine = 128
    freqs = jnp.arange(F, dtype=jnp.int32)[:, None]
    cos_far, sin_far = turn_table(jnp.arange(SEG // fine, dtype=jnp.int32)[None, :] * fine, freqs)
    cos_near, sin_near = turn_table(jnp.arange(fine, dtype=jnp.int32)[None, :], freqs)
    cos_far, sin_far = cos_far[:, :, None], sin_far[:, :, None]
    cos_near, sin_near = cos_near[:, None, :], sin_near[:, None, :]
    cos_sum = cos_far * cos_near - sin_far * sin_near
    sin_sum = -(sin_far * cos_near) - cos_far * sin_near
    return jnp.stack([cos_sum, sin_sum]).astype(jnp.bfloat16).reshape(2 * F, SEG)


def band_rows():
    target = jnp.arange(F, dtype=jnp.int32)[:, None]
    source = jnp.arange(F, dtype=jnp.int32)[None, :]
    inside = jnp.abs(source - target) <= SMOOTH
    counted = (jnp.minimum(target + SMOOTH, F - 1) - jnp.maximum(target - SMOOTH, 0) + 1).astype(
        jnp.float32
    )
    return jnp.where(inside, 1.0 / counted, 0.0)


GROUP = 8
LAG_ROWS = 208
ROWS = 32
STEPS = 16


def lag_rows():
    freqs = jnp.arange(F, dtype=jnp.int32)[None, :]
    shifts = (jnp.arange(LAG_ROWS, dtype=jnp.int32) - MAXLAG)[:, None]
    angle = 2.0 * math.pi / SEG * (freqs * shifts % SEG).astype(jnp.float32)
    factor = 1.0 / math.sqrt(F)
    both = jnp.stack([jnp.cos(angle) * factor, -jnp.sin(angle) * factor], axis=1)
    both = jnp.where(shifts[:, :, None] <= MAXLAG, both, 0.0)
    both = both.reshape(LAG_ROWS, 2, F // GROUP, GROUP).transpose(0, 2, 1, 3)
    return both.reshape(LAG_ROWS, 2 * F).astype(jnp.bfloat16)


def correlate_kernel(*refs):
    place_ref, own_ref, far_ref = refs[:3]
    blocks = refs[3:11]
    own_mask, masks = refs[11], refs[12:16]
    reach_ref, lag_ref, out_ref, cross, lagged, scale_ref = refs[16:]
    chunk = pl.program_id(0)
    step = pl.program_id(1)
    rows = out_ref.shape[0]
    chans = blocks[0].shape[1] // 2
    half_depth = GROUP * own_mask.shape[0]
    depth = 2 * half_depth
    groups = own_ref.shape[0] // half_depth
    per_freq = half_depth // GROUP
    seg_local = per_freq // 2
    cols = 4 * chans
    lane = lax.broadcasted_iota(jnp.int32, (GROUP, depth), 1)
    row = lax.broadcasted_iota(jnp.int32, (GROUP, depth), 0)
    keep = (lax.rem(lane, half_depth) // per_freq == row)[None]

    def pick(value, at):
        part = value[at : at + rows]
        for c in range(1, chans // rows):
            part = jnp.where(chunk == c, value[at + c * rows : at + (c + 1) * rows], part)
        return part

    def one_group(g, carry):
        at = pl.multiple_of(g * half_depth, half_depth)
        tiles = [ref[pl.ds(at, half_depth), :] for ref in blocks]
        own = jnp.concatenate(
            [own_ref[pl.ds(at, half_depth), :], far_ref[pl.ds(at, half_depth), :]], axis=0
        ).astype(jnp.float32)
        split = own.reshape(2 * GROUP, 2, seg_local, 2 * chans)
        swapped = jnp.stack([split[:, 1], -split[:, 0]], axis=1).reshape(depth, 2 * chans)
        pairs, turns = own.T, swapped.T
        for fh in range(2):
            cut = slice(fh * chans, (fh + 1) * chans)
            mine = jnp.concatenate([t[:, cut] for t in tiles[:4]], axis=1)
            other = jnp.concatenate([t[:, cut] for t in tiles[4:]], axis=1)
            weights = jnp.concatenate([mine, other], axis=0)
            pair = pick(pairs, fh * chans)[:, None, :]
            turn = pick(turns, fh * chans)[:, None, :]
            spread = jnp.concatenate(
                [jnp.where(keep, pair, 0.0), jnp.where(keep, turn, 0.0)], axis=1
            )
            spread = spread.reshape(rows * 2 * GROUP, depth).astype(jnp.bfloat16)
            product = jnp.dot(spread, weights, preferred_element_type=jnp.float32)
            place = (fh * groups * pl.num_programs(1) + step * groups + g) * 2 * GROUP
            cross[:, pl.ds(pl.multiple_of(place, 2 * GROUP), 2 * GROUP), :] = product.astype(
                jnp.bfloat16
            ).reshape(rows, 2 * GROUP, cols)
        return carry

    lax.fori_loop(0, groups, one_group, 0)

    @pl.when(step == pl.num_programs(1) - 1)
    def finish():
        mine = pick(own_mask[...].astype(jnp.float32).T, 0)
        theirs = jnp.concatenate([ref[:, :chans] for ref in masks], axis=1)
        counts = jnp.dot(
            mine.astype(jnp.bfloat16), theirs, preferred_element_type=jnp.float32
        )
        first_chan = place_ref[0] + chunk * rows + lax.broadcasted_iota(jnp.int32, (rows, cols), 0)
        second_chan = place_ref[1] + lax.broadcasted_iota(jnp.int32, (rows, cols), 1)
        gap = second_chan - first_chan
        valid = (gap >= 1) & (gap <= reach_ref[...]) & (second_chan < place_ref[2])
        scale_ref[...] = jnp.where(valid, 1.0 / jnp.maximum(counts, 1.0), 0.0)

        def one_row(i, carry):
            value = jnp.dot(lag_ref[...], cross[i], preferred_element_type=jnp.float32)
            value = value * scale_ref[pl.ds(i, 1), :]
            value = jnp.concatenate(
                [value, jnp.zeros((256 - LAG_ROWS, cols), jnp.float32)], axis=0
            )
            lagged[:, pl.ds(i, 1), :] = value.T[:, None, :]
            return carry

        lax.fori_loop(0, rows, one_row, 0)
        lanes = lax.broadcasted_iota(jnp.int32, (rows, 128), 1)

        def span(h, carry):
            base = h * 128
            out_at = h * (128 * LAGS)
            waiting = {}
            for j in range(128):
                tile, shift = divmod(j * LAGS, 128)
                block = lagged[base + j]
                if shift:
                    block = pltpu.roll(block, shift, 1)
                first, second = block[:, :128], block[:, 128:]
                if shift:
                    parts = (
                        jnp.where(lanes >= shift, first, 0.0),
                        second,
                        jnp.where(lanes < shift, first, 0.0),
                    )
                else:
                    parts = (first, second)
                for t, part in enumerate(parts):
                    have = waiting.get(tile + t)
                    waiting[tile + t] = part if have is None else have + part
                upto = (j + 1) * LAGS // 128
                for t in sorted(waiting):
                    if t < upto:
                        done = waiting.pop(t)
                        out_ref[:, pl.ds(pl.multiple_of(out_at + t * 128, 128), 128)] = (
                            done.astype(out_ref.dtype)
                        )
            return carry

        lax.fori_loop(0, cols // 128, span, 0)


def correlate(place, own, own_far, blocks, reach, lags, seg_all):
    num_chan = reach.shape[0]
    rows = min(ROWS, num_chan)
    spec_rows = own.shape[0] - seg_all
    cols = len(blocks) // 2 * num_chan
    blk_spec = pl.BlockSpec((spec_rows // STEPS, 2 * num_chan), lambda i, g: (g, 0))
    mask_spec = pl.BlockSpec((seg_all, 2 * num_chan), lambda i, g: (spec_rows // seg_all, 0))
    return pl.pallas_call(
        correlate_kernel,
        grid=(num_chan // rows, STEPS),
        out_shape=jax.ShapeDtypeStruct((num_chan, cols * LAGS), jnp.bfloat16),
        in_specs=[pl.BlockSpec(memory_space=pltpu.SMEM)]
        + [blk_spec] * 10
        + [mask_spec] * 5
        + [
            pl.BlockSpec((rows, 1), lambda i, g: (i, 0)),
            pl.BlockSpec((LAG_ROWS, 2 * F), lambda i, g: (0, 0)),
        ],
        out_specs=pl.BlockSpec((rows, cols * LAGS), lambda i, g: (i, 0)),
        scratch_shapes=[
            pltpu.VMEM((rows, 2 * F, cols), jnp.bfloat16),
            pltpu.VMEM((cols, rows, 256), jnp.float32),
            pltpu.VMEM((rows, cols), jnp.float32),
        ],
        compiler_params=pltpu.CompilerParams(vmem_limit_bytes=67043328 - 1024 * 1024),
    )(place, own, own_far, *blocks, own, *blocks[: len(blocks) // 2], reach, lags)


def swap_section(value):
    count = lax.axis_size("section")
    return lax.ppermute(value, "section", [(i, count - 1 - i) for i in range(count)])


def fetch(value, route):
    return lax.ppermute(value, "chan", route)


def shards(raw_strain, seg_starts, quality_mask, pair_reach):
    num_chan = raw_strain.shape[0]
    seg_local = seg_starts.shape[0]
    section_idx = lax.axis_index("section")
    chan_idx = lax.axis_index("chan")
    cycle_size = lax.axis_size("chan")
    total_chan = num_chan * cycle_size
    windows = jax.vmap(
        lambda offset: lax.dynamic_slice_in_dim(raw_strain, offset, SEG, 1), out_axes=0
    )(seg_starts)
    centred = windows - jnp.mean(windows, axis=2, keepdims=True)
    tapered = (centred * hann_window()).astype(jnp.bfloat16)
    spectrum = lax.dot_general(
        dft_rows(),
        tapered.reshape(seg_local * num_chan, SEG),
        (((1,), (1,)), ((), ())),
        preferred_element_type=jnp.float32,
    )
    real_part = spectrum[:F]
    imag_part = spectrum[F:]
    smooth = jnp.dot(
        band_rows(), real_part * real_part + imag_part * imag_part, precision=lax.Precision.HIGHEST
    )
    own_rows = lax.dynamic_slice_in_dim(quality_mask, section_idx * seg_local, seg_local, 0).astype(
        jnp.float32
    )
    gain = own_rows.reshape(1, seg_local * num_chan) / jnp.sqrt(smooth + 1e-06)
    white = jnp.stack([real_part * gain, imag_part * gain], axis=1).astype(jnp.bfloat16)
    own = (
        white.reshape(2, F // 2, 2 * seg_local, num_chan)
        .transpose(1, 2, 0, 3)
        .reshape(F * seg_local, 2 * num_chan)
    )
    mask_wire = quality_mask.astype(jnp.bfloat16)
    own = jnp.concatenate([own, jnp.concatenate([mask_wire, mask_wire], axis=1)], axis=0)

    first = section_idx == 0
    odd_pair = (chan_idx // 2) % 2 == 1
    odd = chan_idx % 2 == 1
    chans = range(cycle_size)
    up4 = [(i, i - 4) for i in chans if i >= 4]
    pair_swap = [(i, i ^ 2) for i in chans]
    core_swap = [(i, i ^ 1) for i in chans]
    even_swap = [
        (h * cycle_size + i, (1 - h) * cycle_size + i) for h in range(2) for i in chans if i % 2 == 0
    ]
    own_far, plus4 = lax.optimization_barrier((swap_section(own), fetch(own, up4)))
    a0 = jnp.where(first, own, plus4)
    plus8, plus2, a0_far = lax.optimization_barrier(
        (
            fetch(plus4, up4),
            fetch(jnp.where(odd_pair, own, plus4), pair_swap),
            swap_section(jnp.where(first, plus4, own)),
        )
    )
    a4 = jnp.where(first, plus4, plus8)
    plus6, a4_far = lax.optimization_barrier(
        (
            fetch(jnp.where(odd_pair, plus4, plus8), pair_swap),
            lax.ppermute(jnp.where(first, plus8, plus4), ("section", "chan"), even_swap),
        )
    )
    a2 = jnp.where(first, plus2, plus6)
    a2_far, b1, b3 = lax.optimization_barrier(
        (
            swap_section(jnp.where(first, plus6, plus2)),
            fetch(jnp.where(odd, a0, a2), core_swap),
            fetch(jnp.where(odd, a2, a4), core_swap),
        )
    )
    b1_far = fetch(jnp.where(odd, a0_far, a2_far), core_swap)
    b3_far = fetch(jnp.where(odd, a2_far, a4_far), core_swap)

    stops_here = STOPS // lax.axis_size("section")
    first_chan = chan_idx * num_chan
    first_col = first_chan + section_idx * stops_here * num_chan
    place = jnp.stack([first_chan, first_col, jnp.int32(total_chan)]).astype(jnp.int32)
    return correlate(
        place,
        own,
        own_far,
        (a0, b1, a2, b3, a0_far, b1_far, a2_far, b3_far),
        pair_reach[:, None],
        lag_rows(),
        quality_mask.shape[0],
    )


def solution(mesh):
    placed = (P("chan", "section"), P("section"), P(None, "chan"), P("chan"))
    return jax.shard_map(
        shards, mesh=mesh, in_specs=placed, out_specs=P("chan", "section"), check_vma=False
    )
```

```python
import math

import jax
import jax.numpy as jnp
from jax import lax
from jax.experimental import pallas as pl
from jax.experimental.pallas import tpu as pltpu
from jax.sharding import PartitionSpec as P

SEG = 2048
F = 1024
SMOOTH = 64
MAXLAG = 100
LAGS = 201
STOPS = 8


def hann_window():
    steps = jnp.arange(SEG, dtype=jnp.int32).astype(jnp.float32)
    return 0.5 - 0.5 * jnp.cos(2.0 * math.pi / SEG * steps)


def turn_table(times, freqs):
    angle = 2.0 * math.pi / SEG * (times * freqs % SEG).astype(jnp.float32)
    return jnp.cos(angle), jnp.sin(angle)


def dft_rows():
    fine = 128
    freqs = jnp.arange(F, dtype=jnp.int32)[:, None]
    cos_far, sin_far = turn_table(jnp.arange(SEG // fine, dtype=jnp.int32)[None, :] * fine, freqs)
    cos_near, sin_near = turn_table(jnp.arange(fine, dtype=jnp.int32)[None, :], freqs)
    cos_far, sin_far = cos_far[:, :, None], sin_far[:, :, None]
    cos_near, sin_near = cos_near[:, None, :], sin_near[:, None, :]
    cos_sum = cos_far * cos_near - sin_far * sin_near
    sin_sum = -(sin_far * cos_near) - cos_far * sin_near
    return jnp.stack([cos_sum, sin_sum]).astype(jnp.bfloat16).reshape(2 * F, SEG)


def band_rows():
    target = jnp.arange(F, dtype=jnp.int32)[:, None]
    source = jnp.arange(F, dtype=jnp.int32)[None, :]
    inside = jnp.abs(source - target) <= SMOOTH
    counted = (jnp.minimum(target + SMOOTH, F - 1) - jnp.maximum(target - SMOOTH, 0) + 1).astype(
        jnp.float32
    )
    return jnp.where(inside, 1.0 / counted, 0.0)


GROUP = 8
LAG_ROWS = 208
ROWS = 32
STEPS = 16


def lag_rows():
    freqs = jnp.arange(F, dtype=jnp.int32)[None, :]
    shifts = (jnp.arange(LAG_ROWS, dtype=jnp.int32) - MAXLAG)[:, None]
    angle = 2.0 * math.pi / SEG * (freqs * shifts % SEG).astype(jnp.float32)
    factor = 1.0 / math.sqrt(F)
    both = jnp.stack([jnp.cos(angle) * factor, -jnp.sin(angle) * factor], axis=1)
    both = jnp.where(shifts[:, :, None] <= MAXLAG, both, 0.0)
    both = both.reshape(LAG_ROWS, 2, F // GROUP, GROUP).transpose(0, 2, 1, 3)
    return both.reshape(LAG_ROWS, 2 * F).astype(jnp.bfloat16)


def correlate_kernel(*refs):
    place_ref, own_ref, far_ref = refs[:3]
    blocks = refs[3:11]
    own_mask, masks = refs[11], refs[12:16]
    reach_ref, lag_ref, out_ref, cross, lagged, scale_ref = refs[16:]
    chunk = pl.program_id(0)
    step = pl.program_id(1)
    rows = out_ref.shape[0]
    chans = blocks[0].shape[1] // 2
    half_depth = GROUP * own_mask.shape[0]
    depth = 2 * half_depth
    groups = own_ref.shape[0] // half_depth
    per_freq = half_depth // GROUP
    seg_local = per_freq // 2
    cols = 4 * chans
    lane = lax.broadcasted_iota(jnp.int32, (GROUP, depth), 1)
    row = lax.broadcasted_iota(jnp.int32, (GROUP, depth), 0)
    keep = (lax.rem(lane, half_depth) // per_freq == row)[None]

    def pick(value, at):
        part = value[at : at + rows]
        for c in range(1, chans // rows):
            part = jnp.where(chunk == c, value[at + c * rows : at + (c + 1) * rows], part)
        return part

    def one_group(g, carry):
        at = pl.multiple_of(g * half_depth, half_depth)
        tiles = [ref[pl.ds(at, half_depth), :] for ref in blocks]
        own = jnp.concatenate(
            [own_ref[pl.ds(at, half_depth), :], far_ref[pl.ds(at, half_depth), :]], axis=0
        ).astype(jnp.float32)
        split = own.reshape(2 * GROUP, 2, seg_local, 2 * chans)
        swapped = jnp.stack([split[:, 1], -split[:, 0]], axis=1).reshape(depth, 2 * chans)
        pairs, turns = own.T, swapped.T
        for fh in range(2):
            cut = slice(fh * chans, (fh + 1) * chans)
            mine = jnp.concatenate([t[:, cut] for t in tiles[:4]], axis=1)
            other = jnp.concatenate([t[:, cut] for t in tiles[4:]], axis=1)
            weights = jnp.concatenate([mine, other], axis=0)
            pair = pick(pairs, fh * chans)[:, None, :]
            turn = pick(turns, fh * chans)[:, None, :]
            spread = jnp.concatenate(
                [jnp.where(keep, pair, 0.0), jnp.where(keep, turn, 0.0)], axis=1
            )
            spread = spread.reshape(rows * 2 * GROUP, depth).astype(jnp.bfloat16)
            product = jnp.dot(spread, weights, preferred_element_type=jnp.float32)
            place = (fh * groups * pl.num_programs(1) + step * groups + g) * 2 * GROUP
            cross[:, pl.ds(pl.multiple_of(place, 2 * GROUP), 2 * GROUP), :] = product.astype(
                jnp.bfloat16
            ).reshape(rows, 2 * GROUP, cols)
        return carry

    lax.fori_loop(0, groups, one_group, 0, unroll=2)

    @pl.when(step == pl.num_programs(1) - 1)
    def finish():
        mine = pick(own_mask[...].astype(jnp.float32).T, 0)
        theirs = jnp.concatenate([ref[:, :chans] for ref in masks], axis=1)
        counts = jnp.dot(
            mine.astype(jnp.bfloat16), theirs, preferred_element_type=jnp.float32
        )
        first_chan = place_ref[0] + chunk * rows + lax.broadcasted_iota(jnp.int32, (rows, cols), 0)
        second_chan = place_ref[1] + lax.broadcasted_iota(jnp.int32, (rows, cols), 1)
        gap = second_chan - first_chan
        valid = (gap >= 1) & (gap <= reach_ref[...]) & (second_chan < place_ref[2])
        scale_ref[...] = jnp.where(valid, 1.0 / jnp.maximum(counts, 1.0), 0.0)

        def one_row(i, carry):
            value = jnp.dot(lag_ref[...], cross[i], preferred_element_type=jnp.float32)
            value = value * scale_ref[pl.ds(i, 1), :]
            value = jnp.concatenate(
                [value, jnp.zeros((256 - LAG_ROWS, cols), jnp.float32)], axis=0
            )
            lagged[:, pl.ds(i, 1), :] = value.T[:, None, :]
            return carry

        lax.fori_loop(0, rows, one_row, 0, unroll=2)
        lanes = lax.broadcasted_iota(jnp.int32, (rows, 128), 1)

        def span(h, carry):
            base = h * 128
            out_at = h * (128 * LAGS)
            waiting = {}
            for j in range(128):
                tile, shift = divmod(j * LAGS, 128)
                block = lagged[base + j]
                if shift:
                    block = pltpu.roll(block, shift, 1)
                first, second = block[:, :128], block[:, 128:]
                if shift:
                    parts = (
                        jnp.where(lanes >= shift, first, 0.0),
                        second,
                        jnp.where(lanes < shift, first, 0.0),
                    )
                else:
                    parts = (first, second)
                for t, part in enumerate(parts):
                    have = waiting.get(tile + t)
                    waiting[tile + t] = part if have is None else have + part
                upto = (j + 1) * LAGS // 128
                for t in sorted(waiting):
                    if t < upto:
                        done = waiting.pop(t)
                        out_ref[:, pl.ds(pl.multiple_of(out_at + t * 128, 128), 128)] = (
                            done.astype(out_ref.dtype)
                        )
            return carry

        lax.fori_loop(0, cols // 128, span, 0)


def correlate(place, own, own_far, blocks, reach, lags, seg_all):
    num_chan = reach.shape[0]
    rows = min(ROWS, num_chan)
    spec_rows = own.shape[0] - seg_all
    cols = len(blocks) // 2 * num_chan
    blk_spec = pl.BlockSpec((spec_rows // STEPS, 2 * num_chan), lambda i, g: (g, 0))
    mask_spec = pl.BlockSpec((seg_all, 2 * num_chan), lambda i, g: (spec_rows // seg_all, 0))
    return pl.pallas_call(
        correlate_kernel,
        grid=(num_chan // rows, STEPS),
        out_shape=jax.ShapeDtypeStruct((num_chan, cols * LAGS), jnp.bfloat16),
        in_specs=[pl.BlockSpec(memory_space=pltpu.SMEM)]
        + [blk_spec] * 10
        + [mask_spec] * 5
        + [
            pl.BlockSpec((rows, 1), lambda i, g: (i, 0)),
            pl.BlockSpec((LAG_ROWS, 2 * F), lambda i, g: (0, 0)),
        ],
        out_specs=pl.BlockSpec((rows, cols * LAGS), lambda i, g: (i, 0)),
        scratch_shapes=[
            pltpu.VMEM((rows, 2 * F, cols), jnp.bfloat16),
            pltpu.VMEM((cols, rows, 256), jnp.float32),
            pltpu.VMEM((rows, cols), jnp.float32),
        ],
        compiler_params=pltpu.CompilerParams(vmem_limit_bytes=67043328 - 1024 * 1024),
    )(place, own, own_far, *blocks, own, *blocks[: len(blocks) // 2], reach, lags)


def taper_kernel(starts_ref, raw_ref, hann_ref, out_ref):
    width = SEG + 128
    last = (raw_ref.shape[1] - width) // 128

    def one_window(k, carry):
        start = starts_ref[k]
        at = jnp.minimum(start // 128, last) * 128
        wide = raw_ref[:, pl.ds(pl.multiple_of(at, 128), width)]
        window = pltpu.roll(wide, lax.rem(width - (start - at), width), 1)[:, :SEG]
        centred = window - jnp.mean(window, axis=1, keepdims=True)
        out_ref[k] = (centred * hann_ref[...]).astype(out_ref.dtype)
        return carry

    lax.fori_loop(0, out_ref.shape[0], one_window, 0)


def taper(raw_strain, seg_starts):
    num_chan = raw_strain.shape[0]
    seg_local = seg_starts.shape[0]
    rows = 16
    return pl.pallas_call(
        taper_kernel,
        grid=(num_chan // rows,),
        out_shape=jax.ShapeDtypeStruct((seg_local, num_chan, SEG), jnp.bfloat16),
        in_specs=[
            pl.BlockSpec(memory_space=pltpu.SMEM),
            pl.BlockSpec((rows, raw_strain.shape[1]), lambda i: (i, 0)),
            pl.BlockSpec((1, SEG), lambda i: (0, 0)),
        ],
        out_specs=pl.BlockSpec((seg_local, rows, SEG), lambda i: (0, i, 0)),
    )(seg_starts, raw_strain, hann_window()[None, :])


def whiten_kernel(re_lo, re_hi, im_lo, im_hi, sm_lo, sm_hi, keep_ref, wire_ref, out_ref, packed):
    step = pl.program_id(0)
    rows = re_lo.shape[0]
    per_freq = packed.shape[1]
    chans = packed.shape[2] // 2
    segs = per_freq // 2

    @pl.when(step < pl.num_programs(0) - 1)
    def spectra():
        gain_lo = keep_ref[...] / jnp.sqrt(sm_lo[...] + 1e-06)
        gain_hi = keep_ref[...] / jnp.sqrt(sm_hi[...] + 1e-06)
        for part, (low, high) in enumerate(((re_lo, re_hi), (im_lo, im_hi))):
            low, high = low[...] * gain_lo, high[...] * gain_hi
            for k in range(segs):
                cut = slice(k * chans, (k + 1) * chans)
                packed[:, part * segs + k, :] = jnp.concatenate([low[:, cut], high[:, cut]], axis=1)
        out_ref[...] = packed[...].reshape(rows * per_freq, 2 * chans).astype(out_ref.dtype)

    @pl.when(step == pl.num_programs(0) - 1)
    def masks():
        out_ref[: wire_ref.shape[0], :] = wire_ref[...]


def whiten(spectrum, smooth, keep, wire, seg_local):
    num_chan = wire.shape[1] // 2
    rows = 64
    steps = F // 2 // rows
    width = seg_local * num_chan

    def at(first):
        return pl.BlockSpec((rows, width), lambda i: (first * steps + jnp.minimum(i, steps - 1), 0))

    return pl.pallas_call(
        whiten_kernel,
        grid=(steps + 1,),
        out_shape=jax.ShapeDtypeStruct((F * seg_local + wire.shape[0], 2 * num_chan), jnp.bfloat16),
        in_specs=[at(0), at(1), at(2), at(3), at(0), at(1)]
        + [
            pl.BlockSpec((1, width), lambda i: (0, 0)),
            pl.BlockSpec(wire.shape, lambda i: (0, 0)),
        ],
        out_specs=pl.BlockSpec((rows * 2 * seg_local, 2 * num_chan), lambda i: (i, 0)),
        scratch_shapes=[pltpu.VMEM((rows, 2 * seg_local, 2 * num_chan), jnp.float32)],
    )(spectrum, spectrum, spectrum, spectrum, smooth, smooth, keep, wire)


def swap_section(value):
    count = lax.axis_size("section")
    return lax.ppermute(value, "section", [(i, count - 1 - i) for i in range(count)])


def fetch(value, route):
    return lax.ppermute(value, "chan", route)


def shards(raw_strain, seg_starts, quality_mask, pair_reach):
    num_chan = raw_strain.shape[0]
    seg_local = seg_starts.shape[0]
    section_idx = lax.axis_index("section")
    chan_idx = lax.axis_index("chan")
    cycle_size = lax.axis_size("chan")
    total_chan = num_chan * cycle_size
    tapered = taper(raw_strain, seg_starts)
    spectrum = lax.dot_general(
        dft_rows(),
        tapered.reshape(seg_local * num_chan, SEG),
        (((1,), (1,)), ((), ())),
        preferred_element_type=jnp.float32,
    )
    real_part = spectrum[:F]
    imag_part = spectrum[F:]
    smooth = jnp.dot(
        band_rows(), real_part * real_part + imag_part * imag_part, precision=lax.Precision.HIGHEST
    )
    own_rows = lax.dynamic_slice_in_dim(quality_mask, section_idx * seg_local, seg_local, 0).astype(
        jnp.float32
    )
    mask_wire = quality_mask.astype(jnp.bfloat16)
    own = whiten(
        spectrum,
        smooth,
        own_rows.reshape(1, seg_local * num_chan),
        jnp.concatenate([mask_wire, mask_wire], axis=1),
        seg_local,
    )

    first = section_idx == 0
    odd_pair = (chan_idx // 2) % 2 == 1
    odd = chan_idx % 2 == 1
    chans = range(cycle_size)
    up4 = [(i, i - 4) for i in chans if i >= 4]
    pair_swap = [(i, i ^ 2) for i in chans]
    core_swap = [(i, i ^ 1) for i in chans]
    even_swap = [
        (h * cycle_size + i, (1 - h) * cycle_size + i) for h in range(2) for i in chans if i % 2 == 0
    ]
    own_far, plus4 = lax.optimization_barrier((swap_section(own), fetch(own, up4)))
    a0 = jnp.where(first, own, plus4)
    plus8, plus2, a0_far = lax.optimization_barrier(
        (
            fetch(plus4, up4),
            fetch(jnp.where(odd_pair, own, plus4), pair_swap),
            swap_section(jnp.where(first, plus4, own)),
        )
    )
    a4 = jnp.where(first, plus4, plus8)
    plus6, a4_far = lax.optimization_barrier(
        (
            fetch(jnp.where(odd_pair, plus4, plus8), pair_swap),
            lax.ppermute(jnp.where(first, plus8, plus4), ("section", "chan"), even_swap),
        )
    )
    a2 = jnp.where(first, plus2, plus6)
    a2_far, b1, b3 = lax.optimization_barrier(
        (
            swap_section(jnp.where(first, plus6, plus2)),
            fetch(jnp.where(odd, a0, a2), core_swap),
            fetch(jnp.where(odd, a2, a4), core_swap),
        )
    )
    b1_far = fetch(jnp.where(odd, a0_far, a2_far), core_swap)
    b3_far = fetch(jnp.where(odd, a2_far, a4_far), core_swap)

    stops_here = STOPS // lax.axis_size("section")
    first_chan = chan_idx * num_chan
    first_col = first_chan + section_idx * stops_here * num_chan
    place = jnp.stack([first_chan, first_col, jnp.int32(total_chan)]).astype(jnp.int32)
    return correlate(
        place,
        own,
        own_far,
        (a0, b1, a2, b3, a0_far, b1_far, a2_far, b3_far),
        pair_reach[:, None],
        lag_rows(),
        quality_mask.shape[0],
    )


def solution(mesh):
    placed = (P("chan", "section"), P("section"), P(None, "chan"), P("chan"))
    return jax.shard_map(
        shards, mesh=mesh, in_specs=placed, out_specs=P("chan", "section"), check_vma=False
    )
```
